32 devices in a mesh: member: 2 (over x), ty: 16 (over z, y, core).
Axes of the slice: x: 2, y: 2, z: 4, core: 2. Of those that a mesh axis runs over, the one named last changes fastest.
Arguments:
- fields: float32 [32, 768, 6, 768], P('member', 'ty'), parts along dimension 0, may hold values from -6 to 6
- damp_four: float32 [32], P('member'), parts along dimension 0, may hold values from 0.004 to 0.03
- damp_six: float32 [32], P('member'), parts along dimension 0, may hold values from 0.0008 to 0.006
- metric: float32 [4, 768, 6, 768], P(None, 'ty'), may hold values from 0.1 to 1.9
- seam_table: int32 [6, 4, 3], replicated, may hold values from 0 to 5, as said below
Outputs:
- damped: float32 [32, 768, 6, 768], P('member', 'ty'), parts along dimension 0
The draws below stay inside these ranges and needn't reach their ends.
There are 2 independent parts, one for each index of `member`. The reference program is written for one: setup_inputs(seed, part) draws one part's arguments, and reference() takes and returns one part's arrays. A program takes and returns all parts, laid end to end along the dimension named above; an argument that names none is the same for every part. Nothing has to cross between parts.
Inputs may be any that keep to these rules, and one draw needn't show every extreme that they name: seam_table[f, e] = (g, h, r) joins edge e of face f (edge codes as in the reference program) to edge h of face g; r = 1 when the cells of the two edges run in opposite index order. The table describes the surface of a cube with every face seen from outside: the joining is symmetric, no face is joined to itself, and r is 1 exactly when both edges are among (south, east) or both among (north, west).
All inputs are finite; a program needn't handle non-finite values.
Results may differ from the reference program's by a relative error of at most 0.00005.
Values sent between devices are 32-bit elements; how exact they have to be, the bound alone decides.
A program may use at most 128 MiB of HBM per device.

```python
import math
import jax
import jax.numpy as jnp
import numpy as np

C = 768
FACES = 6
LEV = 16


def vector_cross(first, second):
    return (first[1] * second[2] - first[2] * second[1], first[2] * second[0] - first[0] * second[2], first[0] * second[1] - first[1] * second[0])


def negated(vector):
    return (-vector[0], -vector[1], -vector[2])


def cube_table():
    normals = [(1, 0, 0), (-1, 0, 0), (0, 1, 0), (0, -1, 0), (0, 0, 1), (0, 0, -1)]
    tangents = [(0, 1, 0), (0, 0, 1), (0, 0, 1), (1, 0, 0), (1, 0, 0), (0, 1, 0)]
    outward = []
    for face in range(6):
        along = tangents[face]
        upward = vector_cross(normals[face], along)
        outward.append([negated(upward), along, upward, negated(along)])
    result = np.zeros((6, 4, 2), np.int64)
    for face in range(6):
        for side in range(4):
            other = [g for g in range(6) if normals[g] == outward[face][side]][0]
            other_side = [h for h in range(4) if outward[other][h] == normals[face]][0]
            result[face, side, 0] = other
            result[face, side, 1] = other_side
    return result


def draw_seam_table(key, part):
    joined = cube_table()
    first_key, second_key = jax.random.split(jax.random.fold_in(key, 7))
    relabel = jax.random.permutation(first_key, 6).astype(jnp.int32)
    rotation = jax.random.randint(second_key, (6,), 0, 4).astype(jnp.int32)
    face_ids = np.repeat(np.arange(6), 4)
    side_ids = np.tile(np.arange(4), 6)
    other_face = joined[:, :, 0].reshape(-1)
    other_side = joined[:, :, 1].reshape(-1)
    new_face = relabel[face_ids]
    new_side = (jnp.asarray(side_ids, jnp.int32) + rotation[face_ids]) % 4
    near_face = relabel[other_face]
    near_side = (jnp.asarray(other_side, jnp.int32) + rotation[other_face]) % 4
    flipped = ((new_side < 2) == (near_side < 2)).astype(jnp.int32)
    entries = jnp.stack([near_face, near_side, flipped], axis=-1).astype(jnp.int32)
    return jnp.zeros((6, 4, 3), jnp.int32).at[new_face, new_side].set(entries)


def level_of(key, dims, pieces, low, high):
    def one(position, blocks):
        steps = jax.random.uniform(jax.random.fold_in(jax.random.fold_in(key, 6), position), (blocks,), jnp.float32, low / len(pieces), high / len(pieces))
        return jnp.repeat(jnp.exp(steps), dims[position] // blocks).reshape((-1,) + (1,) * (len(dims) - position - 1))

    gain = one(*pieces[0])
    for cut in pieces[1:]:
        gain = gain * one(*cut)
    return gain


def centred(key, shape, scale, bound, cuts=(), held_as=jnp.bfloat16):
    values = jax.random.normal(key, shape, jnp.float32) * scale
    if len(cuts) > 0:
        values = level_of(key, shape, cuts, -0.22, 0.18) * values
    return jnp.clip(values, min=-bound, max=bound).astype(held_as)


def setup_inputs(seed: int = 0, part: int = 0) -> dict:
    key_list = jax.random.split(jax.random.key(seed), 6)
    part_keys = jax.random.split(jax.random.fold_in(key_list[5], part), 6)
    return {
        "fields": centred(part_keys[0], (LEV, C, FACES, C), 1.0, 6.0, ((1, 16),), jnp.float32),
        "damp_four": jnp.clip(jnp.exp(jax.random.uniform(part_keys[1], (LEV,), jnp.float32, math.log(0.004), math.log(0.03))), 0.004, 0.03),
        "damp_six": jnp.clip(jnp.exp(jax.random.uniform(part_keys[2], (LEV,), jnp.float32, math.log(0.0008), math.log(0.006))), 0.0008, 0.006),
        "metric": jnp.clip(1.0 + 0.18 * jax.random.normal(key_list[3], (4, C, FACES, C), jnp.float32), 0.1, 1.9),
        "seam_table": draw_seam_table(jax.random.fold_in(key_list[5], 71), part),
    }


def edge_cells(source):
    return jnp.stack([source[:, 0], jnp.transpose(source[:, :, :, -1], (0, 2, 1)), source[:, -1], jnp.transpose(source[:, :, :, 0], (0, 2, 1))], axis=2)


def seam_halo(edges, seam_table):
    neighbor = edges[:, seam_table[:, :, 0], seam_table[:, :, 1], :]
    flipped = (seam_table[:, :, 2] == 1)[None, :, :, None]
    return jnp.where(flipped, neighbor[..., ::-1], neighbor)


def laplace(source, metric, seam_table):
    halo_cells = seam_halo(edge_cells(source), seam_table)
    west_cells = jnp.transpose(halo_cells[:, :, 3], (0, 2, 1))[..., None]
    east_cells = jnp.transpose(halo_cells[:, :, 1], (0, 2, 1))[..., None]
    padded_x = jnp.concatenate([west_cells, source, east_cells], axis=3)
    padded_y = jnp.concatenate([halo_cells[:, None, :, 0], source, halo_cells[:, None, :, 2]], axis=1)
    return (metric[0] * (padded_x[..., :-2] - source) + metric[1] * (padded_x[..., 2:] - source)
            + metric[2] * (padded_y[:, :-2] - source) + metric[3] * (padded_y[:, 2:] - source))


def reference(fields, damp_four, damp_six, metric, seam_table):
    second = laplace(fields, metric, seam_table)
    fourth = laplace(second, metric, seam_table)
    sixth = laplace(fourth, metric, seam_table)
    return fields - damp_four[:, None, None, None] * fourth + damp_six[:, None, None, None] * sixth
```

```python
import functools

import jax
import jax.numpy as jnp
from jax import lax
from jax.experimental import pallas as pl
from jax.experimental.pallas import tpu as pltpu
from jax.sharding import PartitionSpec as P

LANES = 128


def exchange(south, north, west, east, seam_table):
    index = lax.axis_index("ty")
    count = lax.axis_size("ty")
    levels, faces, width = south.shape
    rows = west.shape[2]
    below = lax.ppermute(north, "ty", [(i, i + 1) for i in range(count - 1)])
    above = lax.ppermute(south, "ty", [(i + 1, i) for i in range(count - 1)])
    sides = jnp.stack([east, west], axis=2)
    blank = jnp.zeros((levels, faces, 2, width), jnp.float32)
    placed = lax.dynamic_update_slice_in_dim(blank, sides, index * rows, 3)
    first = jnp.where(index == 0, south, 0.0)
    last = jnp.where(index == count - 1, north, 0.0)
    rim = jnp.stack([first, placed[:, :, 0], last, placed[:, :, 1]], axis=2)
    edges = lax.psum(rim, "ty").reshape(levels, faces * 4, width)
    picked = (seam_table[:, :, 0] * 4 + seam_table[:, :, 1]).reshape(faces * 4)
    onehot = (picked[:, None] == jnp.arange(faces * 4, dtype=jnp.int32)[None, :]).astype(jnp.float32)
    near = jnp.einsum("jk,lkc->ljc", onehot, edges, precision=lax.Precision.HIGHEST)
    near = near.reshape(levels, faces, 4, width)
    flipped = (seam_table[:, :, 2] == 1)[None, :, :, None]
    halo = jnp.where(flipped, near[..., ::-1], near)
    start = index * rows
    return (
        jnp.where(index == 0, halo[:, :, 0], below),
        jnp.where(index == count - 1, halo[:, :, 2], above),
        lax.dynamic_slice_in_dim(halo[:, :, 3], start, rows, 2),
        lax.dynamic_slice_in_dim(halo[:, :, 1], start, rows, 2),
    )


def weigh(metric, cells, west, east, south, north):
    return (
        metric[0] * (west - cells)
        + metric[1] * (east - cells)
        + metric[2] * (south - cells)
        + metric[3] * (north - cells)
    )


def join(parts, axis):
    return jnp.concatenate(parts, axis=axis)


def frame_step(frame, halo, metric_rows, metric_cols):
    south, north, west, east = frame
    h_south, h_north, h_west, h_east = halo
    k = south.shape[2] - 1

    def along_x(lines, west_halo, east_halo):
        return (
            join([west_halo[..., None], lines[..., :-1]], 3),
            join([lines[..., 1:], east_halo[..., None]], 3),
        )

    c = south[:, :, :k]
    w, e = along_x(c, h_west[:, :, :k], h_east[:, :, :k])
    new_south = weigh(
        metric_rows[0][:, None, :, :k], c, w, e,
        join([h_south[:, :, None], south[:, :, : k - 1]], 2), south[:, :, 1:],
    )
    c = north[:, :, 1:]
    w, e = along_x(c, h_west[:, :, -k:], h_east[:, :, -k:])
    new_north = weigh(
        metric_rows[1][:, None, :, -k:], c, w, e,
        north[:, :, :-1], join([north[:, :, 2:], h_north[:, :, None]], 2),
    )
    c = west[:, :, :k]
    s, n = along_x(c, h_south[:, :, :k], h_north[:, :, :k])
    new_west = weigh(
        metric_cols[0][:, None, :, :k], c,
        join([h_west[:, :, None], west[:, :, : k - 1]], 2), west[:, :, 1:], s, n,
    )
    c = east[:, :, 1:]
    s, n = along_x(c, h_south[:, :, -k:], h_north[:, :, -k:])
    new_east = weigh(
        metric_cols[1][:, None, :, -k:], c,
        east[:, :, :-1], join([east[:, :, 2:], h_east[:, :, None]], 2), s, n,
    )
    return new_south, new_north, new_west, new_east


def halos_of(fields, metric, seam_table):
    def rim(array, k):
        return (
            array[:, :, :k],
            array[:, :, -k:],
            jnp.swapaxes(array[..., :k], 2, 3),
            jnp.swapaxes(array[..., -k:], 2, 3),
        )

    m_south, m_north, m_west, m_east = rim(metric, 2)
    frame = rim(fields, 3)
    rounds = []
    for step in range(3):
        south, north, west, east = frame
        halo = exchange(south[:, :, 0], north[:, :, -1], west[:, :, 0], east[:, :, -1], seam_table)
        rounds.append(halo)
        if step < 2:
            frame = frame_step(frame, halo, (m_south, m_north), (m_west, m_east))
    return rounds


def damp_kernel(four_ref, six_ref, v_ref, m_ref, hr_ref, hc_ref, o_ref, second_ref, fourth_ref):
    block, _, rows, width = v_ref.shape
    tiles = width // LANES
    levels = four_ref.shape[0]
    lane = lax.broadcasted_iota(jnp.int32, (rows, LANES), 1)
    row = lax.broadcasted_iota(jnp.int32, (rows, LANES), 0)
    aligned = rows % 8 == 0

    def at(t):
        return pl.ds(t * LANES, LANES)

    def one_level(j, carry):
        level = pl.program_id(1) * block + j

        def laplace(load, step, put):
            sides = hc_ref[0]
            before = pltpu.roll(sides, lax.rem(2 * LANES - 2 * step * levels - level, LANES), 1)
            beyond = pltpu.roll(
                sides, lax.rem(3 * LANES - 1 - (2 * step + 1) * levels - level, LANES), 1
            )
            right = [pltpu.roll(load(t), 1, 1) for t in range(tiles)]
            for t in range(tiles):
                c = load(t)
                left = pltpu.roll(c, LANES - 1, 1)
                after = pltpu.roll(load(t + 1), LANES - 1, 1) if t + 1 < tiles else beyond
                west = jnp.where(lane == 0, right[t - 1] if t > 0 else before, right[t])
                east = jnp.where(lane == LANES - 1, after, left)
                low = hr_ref[j, 0, 2 * step : 2 * step + 1, at(t)]
                high = hr_ref[j, 0, 2 * step + 1 : 2 * step + 2, at(t)]
                if aligned:
                    south = jnp.where(row == 0, low, pltpu.roll(c, 1, 0))
                    north = jnp.where(row == rows - 1, high, pltpu.roll(c, rows - 1, 0))
                else:
                    south = jnp.concatenate([low, c[:-1]], axis=0)
                    north = jnp.concatenate([c[1:], high], axis=0)
                put(
                    t,
                    m_ref[0, 0, :, at(t)] * (west - c)
                    + m_ref[1, 0, :, at(t)] * (east - c)
                    + m_ref[2, 0, :, at(t)] * (south - c)
                    + m_ref[3, 0, :, at(t)] * (north - c),
                )

        def put_second(t, x):
            second_ref[:, at(t)] = x

        def put_fourth(t, x):
            fourth_ref[:, at(t)] = x

        def put_out(t, x):
            o_ref[j, 0, :, at(t)] = (
                v_ref[j, 0, :, at(t)] - four_ref[level] * fourth_ref[:, at(t)] + six_ref[level] * x
            )

        laplace(lambda t: v_ref[j, 0, :, at(t)], 0, put_second)
        laplace(lambda t: second_ref[:, at(t)], 1, put_fourth)
        laplace(lambda t: fourth_ref[:, at(t)], 2, put_out)
        return carry

    lax.fori_loop(0, block, one_level, 0)


def damp(fields, damp_four, damp_six, metric, halo_rows, halo_cols):
    levels, faces, rows, width = fields.shape
    block = next(b for b in (4, 2, 1) if levels % b == 0)
    cells = fields.size
    return pl.pallas_call(
        damp_kernel,
        grid=(faces, levels // block),
        in_specs=[
            pl.BlockSpec(memory_space=pltpu.SMEM),
            pl.BlockSpec(memory_space=pltpu.SMEM),
            pl.BlockSpec((block, 1, rows, width), lambda f, l: (l, f, 0, 0)),
            pl.BlockSpec((4, 1, rows, width), lambda f, l: (0, f, 0, 0)),
            pl.BlockSpec((block, 1, 8, width), lambda f, l: (l, f, 0, 0)),
            pl.BlockSpec((1, rows, LANES), lambda f, l: (f, 0, 0)),
        ],
        out_specs=pl.BlockSpec((block, 1, rows, width), lambda f, l: (l, f, 0, 0)),
        out_shape=jax.ShapeDtypeStruct(fields.shape, jnp.float32),
        scratch_shapes=[
            pltpu.VMEM((rows, width), jnp.float32),
            pltpu.VMEM((rows, width), jnp.float32),
        ],
        cost_estimate=pl.CostEstimate(flops=40 * cells, bytes_accessed=10 * cells, transcendentals=0),
        name="damp",
    )(damp_four, damp_six, fields, metric, halo_rows, halo_cols)


def per_device(fields, damp_four, damp_six, metric, seam_table):
    fields = jnp.transpose(fields, (0, 2, 1, 3))
    metric = jnp.transpose(metric, (0, 2, 1, 3))
    levels, faces, rows, width = fields.shape
    rounds = halos_of(fields, metric, seam_table)
    halo_rows = jnp.stack([part for halo in rounds for part in halo[:2]], axis=2)
    halo_rows = jnp.pad(halo_rows, ((0, 0), (0, 0), (0, 2), (0, 0)))
    halo_cols = jnp.stack([part for halo in rounds for part in halo[2:]], axis=0)
    halo_cols = jnp.transpose(halo_cols, (2, 3, 0, 1)).reshape(faces, rows, 6 * levels)
    halo_cols = jnp.pad(halo_cols, ((0, 0), (0, 0), (0, LANES - 6 * levels)))
    damped = damp(fields, damp_four, damp_six, metric, halo_rows, halo_cols)
    return jnp.transpose(damped, (0, 2, 1, 3))


def solution(mesh):
    placed = (
        P("member", "ty", None, None),
        P("member"),
        P("member"),
        P(None, "ty", None, None),
        P(),
    )
    return jax.shard_map(
        per_device,
        mesh=mesh,
        in_specs=placed,
        out_specs=P("member", "ty", None, None),
        check_vma=False,
    )
```

```python
import functools

import jax
import jax.numpy as jnp
from jax import lax
from jax.experimental import pallas as pl
from jax.experimental.pallas import tpu as pltpu
from jax.sharding import PartitionSpec as P

LANES = 128


def exchange_kernel(
    count, south, north, sides, pieces, below, above, mirror, first, last, rim, far,
    send, receive, rim_send, rim_receive, piece_send,
):
    me = lax.axis_index("ty")
    end = count - 1

    def copy(source, target, send_sem, receive_sem, device):
        return pltpu.make_async_remote_copy(
            src_ref=source,
            dst_ref=target,
            send_sem=send_sem,
            recv_sem=receive_sem,
            device_id={"ty": device},
            device_id_type=pl.DeviceIdType.MESH,
        )

    upward = copy(north, below, send.at[0], receive.at[0], lax.rem(me + 1, count))
    downward = copy(south, above, send.at[1], receive.at[1], lax.rem(me + end, count))
    across = copy(sides, mirror, send.at[2], receive.at[2], end - me)
    to_first = copy(sides, rim.at[me], rim_send.at[0], rim_receive.at[me], 0)
    to_last = copy(sides, rim.at[me], rim_send.at[1], rim_receive.at[me], end)
    far_last = copy(south, far, send.at[3], receive.at[3], end)
    far_first = copy(north, far, send.at[3], receive.at[3], 0)

    def from_first(d):
        return copy(pieces.at[d], first, piece_send.at[d], receive.at[4], d)

    def from_last(d):
        return copy(pieces.at[d], last, piece_send.at[d], receive.at[5], d)

    def each(low, high, act):
        def body(d, carry):
            act(d)
            return carry

        lax.fori_loop(low, high, body, 0)

    def incoming(d):
        return copy(sides, rim.at[d], rim_send.at[0], rim_receive.at[d], 0)

    @pl.when(me > 0)
    def _():
        to_first.start()
        downward.start()

    @pl.when(me < end)
    def _():
        to_last.start()
        upward.start()

    @pl.when(me == 0)
    def _():
        far_last.start()
        each(1, count, lambda d: from_first(d).start())

    @pl.when(me == end)
    def _():
        far_first.start()
        each(0, end, lambda d: from_last(d).start())

    across.start()
    across.wait()

    @pl.when(me > 0)
    def _():
        to_first.wait_send()
        downward.wait_send()
        upward.wait_recv()
        from_first(me).wait_recv()

    @pl.when(me < end)
    def _():
        to_last.wait_send()
        upward.wait_send()
        downward.wait_recv()
        from_last(me).wait_recv()

    @pl.when(me == 0)
    def _():
        far_last.wait_send()
        far_first.wait_recv()
        each(1, count, lambda d: from_first(d).wait_send())
        each(1, count, lambda d: incoming(d).wait_recv())

    @pl.when(me == end)
    def _():
        far_first.wait_send()
        far_last.wait_recv()
        each(0, end, lambda d: from_last(d).wait_send())
        each(0, end, lambda d: incoming(d).wait_recv())


def choose(picked, lines):
    onehot = (picked[:, None] == jnp.arange(lines.shape[1], dtype=jnp.int32)[None, :]).astype(jnp.float32)
    return jnp.einsum("jk,lkc->ljc", onehot, lines, precision=lax.Precision.HIGHEST)


def exchange(south, north, west, east, seam_table):
    index = lax.axis_index("ty")
    count = lax.axis_size("ty")
    levels, faces, width = south.shape
    rows = west.shape[2]
    lines = levels * faces
    packed = -(-2 * rows // LANES) * LANES
    at_first = index == 0
    at_last = index == count - 1
    south_flat = south.reshape(lines, width)
    north_flat = north.reshape(lines, width)
    spare = ((0, 0), (0, packed - 2 * rows))
    sides = jnp.pad(join([east.reshape(lines, rows), west.reshape(lines, rows)], 1), spare)
    cut = jnp.swapaxes(jnp.where(at_first, south_flat, north_flat).reshape(lines, count, rows), 0, 1)
    pieces = jnp.pad(join([cut, cut[::-1]], 2), ((0, 0),) + spare)
    row_shape = jax.ShapeDtypeStruct((lines, width), jnp.float32)
    piece_shape = jax.ShapeDtypeStruct((lines, packed), jnp.float32)
    anywhere = pl.BlockSpec(memory_space=pl.ANY)
    below, above, mirror, first, last, rim, far = pl.pallas_call(
        functools.partial(exchange_kernel, count),
        out_shape=(
            row_shape, row_shape, piece_shape, piece_shape, piece_shape,
            jax.ShapeDtypeStruct((count, lines, packed), jnp.float32), row_shape,
        ),
        in_specs=[anywhere] * 4,
        out_specs=(anywhere,) * 7,
        scratch_shapes=[
            pltpu.SemaphoreType.DMA((4,)),
            pltpu.SemaphoreType.DMA((6,)),
            pltpu.SemaphoreType.DMA((2,)),
            pltpu.SemaphoreType.DMA((count,)),
            pltpu.SemaphoreType.DMA((count,)),
        ],
        compiler_params=pltpu.CompilerParams(has_side_effects=True),
        name="exchange",
    )(south_flat, north_flat, sides, pieces)
    first = jnp.where(at_first, pieces[0], first)
    last = jnp.where(at_last, pieces[count - 1], last)

    def near_lines(begin):
        part = slice(begin, begin + rows)
        own = sides if begin == 0 else mirror
        return join(
            [
                first[:, None, part], own[:, None, :rows],
                last[:, None, part], own[:, None, rows : 2 * rows],
            ],
            1,
        ).reshape(levels, faces * 4, rows)

    picked = seam_table[:, :, 0] * 4 + seam_table[:, :, 1]
    side_pick = (picked + faces * 4 * seam_table[:, :, 2])[:, 1::2].reshape(faces * 2)
    nearby = join([near_lines(0), near_lines(rows)[..., ::-1]], 1)
    side_halo = choose(side_pick, nearby).reshape(levels, faces, 2, rows)

    mine = (jnp.arange(count) == index)[:, None, None]
    rim = jnp.swapaxes(jnp.where(mine, sides[None], rim), 0, 1)
    edges = jnp.stack(
        [
            jnp.where(at_first, south_flat, far),
            rim[:, :, :rows].reshape(lines, width),
            jnp.where(at_first, far, north_flat),
            rim[:, :, rows : 2 * rows].reshape(lines, width),
        ],
        axis=1,
    ).reshape(levels, faces * 4, width)
    end_table = jnp.where(at_first, seam_table[:, 0], seam_table[:, 2])
    row = choose(end_table[:, 0] * 4 + end_table[:, 1], edges)
    row = jnp.where((end_table[:, 2] == 1)[None, :, None], row[..., ::-1], row)
    return (
        jnp.where(at_first, row, below.reshape(south.shape)),
        jnp.where(at_last, row, above.reshape(south.shape)),
        side_halo[:, :, 1],
        side_halo[:, :, 0],
    )


def weigh(metric, cells, west, east, south, north):
    return (
        metric[0] * (west - cells)
        + metric[1] * (east - cells)
        + metric[2] * (south - cells)
        + metric[3] * (north - cells)
    )


def join(parts, axis):
    return jnp.concatenate(parts, axis=axis)


def frame_step(frame, halo, metric_rows, metric_cols):
    south, north, west, east = frame
    h_south, h_north, h_west, h_east = halo
    k = south.shape[2] - 1

    def along_x(lines, west_halo, east_halo):
        return (
            join([west_halo[..., None], lines[..., :-1]], 3),
            join([lines[..., 1:], east_halo[..., None]], 3),
        )

    c = south[:, :, :k]
    w, e = along_x(c, h_west[:, :, :k], h_east[:, :, :k])
    new_south = weigh(
        metric_rows[0][:, None, :, :k], c, w, e,
        join([h_south[:, :, None], south[:, :, : k - 1]], 2), south[:, :, 1:],
    )
    c = north[:, :, 1:]
    w, e = along_x(c, h_west[:, :, -k:], h_east[:, :, -k:])
    new_north = weigh(
        metric_rows[1][:, None, :, -k:], c, w, e,
        north[:, :, :-1], join([north[:, :, 2:], h_north[:, :, None]], 2),
    )
    c = west[:, :, :k]
    s, n = along_x(c, h_south[:, :, :k], h_north[:, :, :k])
    new_west = weigh(
        metric_cols[0][:, None, :, :k], c,
        join([h_west[:, :, None], west[:, :, : k - 1]], 2), west[:, :, 1:], s, n,
    )
    c = east[:, :, 1:]
    s, n = along_x(c, h_south[:, :, -k:], h_north[:, :, -k:])
    new_east = weigh(
        metric_cols[1][:, None, :, -k:], c,
        east[:, :, :-1], join([east[:, :, 2:], h_east[:, :, None]], 2), s, n,
    )
    return new_south, new_north, new_west, new_east


def halos_of(fields, metric, seam_table):
    def rim(array, k):
        return (
            array[:, :, :k],
            array[:, :, -k:],
            jnp.swapaxes(array[..., :k], 2, 3),
            jnp.swapaxes(array[..., -k:], 2, 3),
        )

    m_south, m_north, m_west, m_east = rim(metric, 2)
    frame = rim(fields, 3)
    rounds = []
    for step in range(3):
        south, north, west, east = frame
        halo = exchange(south[:, :, 0], north[:, :, -1], west[:, :, 0], east[:, :, -1], seam_table)
        rounds.append(halo)
        if step < 2:
            frame = frame_step(frame, halo, (m_south, m_north), (m_west, m_east))
    return rounds


def damp_kernel(four_ref, six_ref, v_ref, m_ref, hr_ref, hc_ref, o_ref, second_ref, fourth_ref):
    block, _, rows, width = v_ref.shape
    tiles = width // LANES
    levels = four_ref.shape[0]
    lane = lax.broadcasted_iota(jnp.int32, (rows, LANES), 1)
    row = lax.broadcasted_iota(jnp.int32, (rows, LANES), 0)
    aligned = rows % 8 == 0

    def at(t):
        return pl.ds(t * LANES, LANES)

    def one_level(j, carry):
        level = pl.program_id(1) * block + j

        def laplace(load, step, put):
            sides = hc_ref[0]
            before = pltpu.roll(sides, lax.rem(2 * LANES - 2 * step * levels - level, LANES), 1)
            beyond = pltpu.roll(
                sides, lax.rem(3 * LANES - 1 - (2 * step + 1) * levels - level, LANES), 1
            )
            right, left = before, pltpu.roll(load(0), LANES - 1, 1)
            for t in range(tiles):
                c = load(t)
                prior, right = right, pltpu.roll(c, 1, 1)
                after = pltpu.roll(load(t + 1), LANES - 1, 1) if t + 1 < tiles else beyond
                west = jnp.where(lane == 0, prior, right)
                east = jnp.where(lane == LANES - 1, after, left)
                left = after
                low = hr_ref[j, 0, 2 * step : 2 * step + 1, at(t)]
                high = hr_ref[j, 0, 2 * step + 1 : 2 * step + 2, at(t)]
                if aligned:
                    south = jnp.where(row == 0, low, pltpu.roll(c, 1, 0))
                    north = jnp.where(row == rows - 1, high, pltpu.roll(c, rows - 1, 0))
                else:
                    south = jnp.concatenate([low, c[:-1]], axis=0)
                    north = jnp.concatenate([c[1:], high], axis=0)
                put(
                    t,
                    m_ref[0, 0, :, at(t)] * (west - c)
                    + m_ref[1, 0, :, at(t)] * (east - c)
                    + m_ref[2, 0, :, at(t)] * (south - c)
                    + m_ref[3, 0, :, at(t)] * (north - c),
                )

        def put_second(t, x):
            second_ref[:, at(t)] = x

        def put_fourth(t, x):
            fourth_ref[:, at(t)] = x

        def put_out(t, x):
            o_ref[j, 0, :, at(t)] = (
                v_ref[j, 0, :, at(t)] - four_ref[level] * fourth_ref[:, at(t)] + six_ref[level] * x
            )

        laplace(lambda t: v_ref[j, 0, :, at(t)], 0, put_second)
        laplace(lambda t: second_ref[:, at(t)], 1, put_fourth)
        laplace(lambda t: fourth_ref[:, at(t)], 2, put_out)
        return carry

    lax.fori_loop(0, block, one_level, 0)


def damp(fields, damp_four, damp_six, metric, halo_rows, halo_cols):
    levels, faces, rows, width = fields.shape
    block = next(b for b in (4, 2, 1) if levels % b == 0)
    cells = fields.size
    return pl.pallas_call(
        damp_kernel,
        grid=(faces, levels // block),
        in_specs=[
            pl.BlockSpec(memory_space=pltpu.SMEM),
            pl.BlockSpec(memory_space=pltpu.SMEM),
            pl.BlockSpec((block, 1, rows, width), lambda f, l: (l, f, 0, 0)),
            pl.BlockSpec((4, 1, rows, width), lambda f, l: (0, f, 0, 0)),
            pl.BlockSpec((block, 1, 8, width), lambda f, l: (l, f, 0, 0)),
            pl.BlockSpec((1, rows, LANES), lambda f, l: (f, 0, 0)),
        ],
        out_specs=pl.BlockSpec((block, 1, rows, width), lambda f, l: (l, f, 0, 0)),
        out_shape=jax.ShapeDtypeStruct(fields.shape, jnp.float32),
        scratch_shapes=[
            pltpu.VMEM((rows, width), jnp.float32),
            pltpu.VMEM((rows, width), jnp.float32),
        ],
        cost_estimate=pl.CostEstimate(flops=40 * cells, bytes_accessed=10 * cells, transcendentals=0),
        name="damp",
    )(damp_four, damp_six, fields, metric, halo_rows, halo_cols)


def per_device(fields, damp_four, damp_six, metric, seam_table):
    fields = jnp.transpose(fields, (0, 2, 1, 3))
    metric = jnp.transpose(metric, (0, 2, 1, 3))
    levels, faces, rows, width = fields.shape
    rounds = halos_of(fields, metric, seam_table)
    halo_rows = jnp.stack([part for halo in rounds for part in halo[:2]], axis=2)
    halo_rows = jnp.pad(halo_rows, ((0, 0), (0, 0), (0, 2), (0, 0)))
    halo_cols = jnp.stack([part for halo in rounds for part in halo[2:]], axis=0)
    halo_cols = jnp.transpose(halo_cols, (2, 3, 0, 1)).reshape(faces, rows, 6 * levels)
    halo_cols = jnp.pad(halo_cols, ((0, 0), (0, 0), (0, LANES - 6 * levels)))
    damped = damp(fields, damp_four, damp_six, metric, halo_rows, halo_cols)
    return jnp.transpose(damped, (0, 2, 1, 3))


def solution(mesh):
    placed = (
        P("member", "ty", None, None),
        P("member"),
        P("member"),
        P(None, "ty", None, None),
        P(),
    )
    return jax.shard_map(
        per_device,
        mesh=mesh,
        in_specs=placed,
        out_specs=P("member", "ty", None, None),
        check_vma=False,
    )
```

```python
import functools

import jax
import jax.numpy as jnp
from jax import lax
from jax.experimental import pallas as pl
from jax.experimental.pallas import tpu as pltpu
from jax.sharding import PartitionSpec as P

LANES = 128


def exchange_kernel(
    count, south, north, sides, pieces, below, above, mirror, first, last, rim, far,
    send, receive, rim_send, rim_receive, piece_send,
):
    me = lax.axis_index("ty")
    end = count - 1

    def copy(source, target, send_sem, receive_sem, device):
        return pltpu.make_async_remote_copy(
            src_ref=source,
            dst_ref=target,
            send_sem=send_sem,
            recv_sem=receive_sem,
            device_id={"ty": device},
            device_id_type=pl.DeviceIdType.MESH,
        )

    upward = copy(north, below, send.at[0], receive.at[0], lax.rem(me + 1, count))
    downward = copy(south, above, send.at[1], receive.at[1], lax.rem(me + end, count))
    across = copy(sides, mirror, send.at[2], receive.at[2], end - me)
    to_first = copy(sides, rim.at[me], rim_send.at[0], rim_receive.at[me], 0)
    to_last = copy(sides, rim.at[me], rim_send.at[1], rim_receive.at[me], end)
    far_last = copy(south, far, send.at[3], receive.at[3], end)
    far_first = copy(north, far, send.at[3], receive.at[3], 0)

    def from_first(d):
        return copy(pieces.at[d], first, piece_send.at[d], receive.at[4], d)

    def from_last(d):
        return copy(pieces.at[d], last, piece_send.at[d], receive.at[5], d)

    def each(low, high, act):
        def body(d, carry):
            act(d)
            return carry

        lax.fori_loop(low, high, body, 0)

    def incoming(d):
        return copy(sides, rim.at[d], rim_send.at[0], rim_receive.at[d], 0)

    @pl.when(me > 0)
    def _():
        to_first.start()
        downward.start()

    @pl.when(me < end)
    def _():
        to_last.start()
        upward.start()

    @pl.when(me == 0)
    def _():
        far_last.start()
        each(1, count, lambda d: from_first(d).start())

    @pl.when(me == end)
    def _():
        far_first.start()
        each(0, end, lambda d: from_last(d).start())

    across.start()
    across.wait()

    @pl.when(me > 0)
    def _():
        to_first.wait_send()
        downward.wait_send()
        upward.wait_recv()
        from_first(me).wait_recv()

    @pl.when(me < end)
    def _():
        to_last.wait_send()
        upward.wait_send()
        downward.wait_recv()
        from_last(me).wait_recv()

    @pl.when(me == 0)
    def _():
        far_last.wait_send()
        far_first.wait_recv()
        each(1, count, lambda d: from_first(d).wait_send())
        each(1, count, lambda d: incoming(d).wait_recv())

    @pl.when(me == end)
    def _():
        far_first.wait_send()
        far_last.wait_recv()
        each(0, end, lambda d: from_last(d).wait_send())
        each(0, end, lambda d: incoming(d).wait_recv())


def choose(edge, face, lines):
    edges, faces = lines.shape[0], lines.shape[2]
    hit_edge = edge[:, None, None] == jnp.arange(edges, dtype=jnp.int32)[None, :, None]
    hit_face = face[:, None, None] == jnp.arange(faces, dtype=jnp.int32)[None, None, :]
    onehot = (hit_edge & hit_face).astype(jnp.float32)
    return jnp.einsum("jhg,hlgc->ljc", onehot, lines, precision=lax.Precision.HIGHEST)


def exchange(south, north, west, east, seam_table):
    index = lax.axis_index("ty")
    count = lax.axis_size("ty")
    levels, faces, width = south.shape
    rows = west.shape[2]
    lines = levels * faces
    packed = -(-2 * rows // LANES) * LANES
    at_first = index == 0
    at_last = index == count - 1
    south_flat = south.reshape(lines, width)
    north_flat = north.reshape(lines, width)
    spare = ((0, 0), (0, packed - 2 * rows))
    sides = jnp.pad(join([east.reshape(lines, rows), west.reshape(lines, rows)], 1), spare)
    cut = jnp.swapaxes(jnp.where(at_first, south_flat, north_flat).reshape(lines, count, rows), 0, 1)
    pieces = jnp.pad(join([cut, cut[::-1]], 2), ((0, 0),) + spare)
    row_shape = jax.ShapeDtypeStruct((lines, width), jnp.float32)
    piece_shape = jax.ShapeDtypeStruct((lines, packed), jnp.float32)
    anywhere = pl.BlockSpec(memory_space=pl.ANY)
    below, above, mirror, first, last, rim, far = pl.pallas_call(
        functools.partial(exchange_kernel, count),
        out_shape=(
            row_shape, row_shape, piece_shape, piece_shape, piece_shape,
            jax.ShapeDtypeStruct((count, lines, packed), jnp.float32), row_shape,
        ),
        in_specs=[anywhere] * 4,
        out_specs=(anywhere,) * 7,
        scratch_shapes=[
            pltpu.SemaphoreType.DMA((4,)),
            pltpu.SemaphoreType.DMA((6,)),
            pltpu.SemaphoreType.DMA((2,)),
            pltpu.SemaphoreType.DMA((count,)),
            pltpu.SemaphoreType.DMA((count,)),
        ],
        compiler_params=pltpu.CompilerParams(has_side_effects=True),
        name="exchange",
    )(south_flat, north_flat, sides, pieces)
    first = jnp.where(at_first, pieces[0], first)
    last = jnp.where(at_last, pieces[count - 1], last)

    def near_lines(begin):
        part = slice(begin, begin + rows)
        own = sides if begin == 0 else mirror
        return jnp.stack([first[:, part], own[:, :rows], last[:, part], own[:, rows : 2 * rows]])

    nearby = join([near_lines(0), near_lines(rows)[..., ::-1]], 0).reshape(8, levels, faces, rows)
    side_table = seam_table[:, 1::2].reshape(faces * 2, 3)
    side_halo = choose(side_table[:, 1] + 4 * side_table[:, 2], side_table[:, 0], nearby)
    side_halo = side_halo.reshape(levels, faces, 2, rows)

    mine = (jnp.arange(count) == index)[:, None, None]
    rim = jnp.swapaxes(jnp.where(mine, sides[None], rim), 0, 1)
    edges = jnp.stack(
        [
            jnp.where(at_first, south_flat, far),
            rim[:, :, :rows].reshape(lines, width),
            jnp.where(at_first, far, north_flat),
            rim[:, :, rows : 2 * rows].reshape(lines, width),
        ]
    ).reshape(4, levels, faces, width)
    end_table = jnp.where(at_first, seam_table[:, 0], seam_table[:, 2])
    row = choose(end_table[:, 1], end_table[:, 0], edges)
    row = jnp.where((end_table[:, 2] == 1)[None, :, None], row[..., ::-1], row)
    return (
        jnp.where(at_first, row, below.reshape(south.shape)),
        jnp.where(at_last, row, above.reshape(south.shape)),
        side_halo[:, :, 1],
        side_halo[:, :, 0],
    )


def weigh(metric, cells, west, east, south, north):
    return (
        metric[0] * (west - cells)
        + metric[1] * (east - cells)
        + metric[2] * (south - cells)
        + metric[3] * (north - cells)
    )


def join(parts, axis):
    return jnp.concatenate(parts, axis=axis)


def frame_step(frame, halo, metric_rows, metric_cols):
    south, north, west, east = frame
    h_south, h_north, h_west, h_east = halo
    k = south.shape[2] - 1

    def along_x(lines, west_halo, east_halo):
        return (
            join([west_halo[..., None], lines[..., :-1]], 3),
            join([lines[..., 1:], east_halo[..., None]], 3),
        )

    c = south[:, :, :k]
    w, e = along_x(c, h_west[:, :, :k], h_east[:, :, :k])
    new_south = weigh(
        metric_rows[0][:, None, :, :k], c, w, e,
        join([h_south[:, :, None], south[:, :, : k - 1]], 2), south[:, :, 1:],
    )
    c = north[:, :, 1:]
    w, e = along_x(c, h_west[:, :, -k:], h_east[:, :, -k:])
    new_north = weigh(
        metric_rows[1][:, None, :, -k:], c, w, e,
        north[:, :, :-1], join([north[:, :, 2:], h_north[:, :, None]], 2),
    )
    c = west[:, :, :k]
    s, n = along_x(c, h_south[:, :, :k], h_north[:, :, :k])
    new_west = weigh(
        metric_cols[0][:, None, :, :k], c,
        join([h_west[:, :, None], west[:, :, : k - 1]], 2), west[:, :, 1:], s, n,
    )
    c = east[:, :, 1:]
    s, n = along_x(c, h_south[:, :, -k:], h_north[:, :, -k:])
    new_east = weigh(
        metric_cols[1][:, None, :, -k:], c,
        east[:, :, :-1], join([east[:, :, 2:], h_east[:, :, None]], 2), s, n,
    )
    return new_south, new_north, new_west, new_east


def halos_of(fields, metric, seam_table):
    def rim(array, k):
        return (
            array[:, :, :k],
            array[:, :, -k:],
            jnp.swapaxes(array[..., :k], 2, 3),
            jnp.swapaxes(array[..., -k:], 2, 3),
        )

    m_south, m_north, m_west, m_east = rim(metric, 2)
    frame = rim(fields, 3)
    rounds = []
    for step in range(3):
        south, north, west, east = frame
        halo = exchange(south[:, :, 0], north[:, :, -1], west[:, :, 0], east[:, :, -1], seam_table)
        rounds.append(halo)
        if step < 2:
            frame = frame_step(frame, halo, (m_south, m_north), (m_west, m_east))
    return rounds


def damp_kernel(four_ref, six_ref, v_ref, m_ref, hr_ref, hc_ref, o_ref, second_ref, fourth_ref):
    block, _, rows, width = v_ref.shape
    tiles = width // LANES
    levels = four_ref.shape[0]
    lane = lax.broadcasted_iota(jnp.int32, (rows, LANES), 1)
    row = lax.broadcasted_iota(jnp.int32, (rows, LANES), 0)
    aligned = rows % 8 == 0

    def at(t):
        return pl.ds(t * LANES, LANES)

    def one_level(j, carry):
        level = pl.program_id(1) * block + j

        def laplace(load, step, put):
            sides = hc_ref[0]
            before = pltpu.roll(sides, lax.rem(2 * LANES - 2 * step * levels - level, LANES), 1)
            beyond = pltpu.roll(
                sides, lax.rem(3 * LANES - 1 - (2 * step + 1) * levels - level, LANES), 1
            )
            right, left = before, pltpu.roll(load(0), LANES - 1, 1)
            for t in range(tiles):
                c = load(t)
                prior, right = right, pltpu.roll(c, 1, 1)
                after = pltpu.roll(load(t + 1), LANES - 1, 1) if t + 1 < tiles else beyond
                west = jnp.where(lane == 0, prior, right)
                east = jnp.where(lane == LANES - 1, after, left)
                left = after
                low = hr_ref[j, 0, 2 * step : 2 * step + 1, at(t)]
                high = hr_ref[j, 0, 2 * step + 1 : 2 * step + 2, at(t)]
                if aligned:
                    south = jnp.where(row == 0, low, pltpu.roll(c, 1, 0))
                    north = jnp.where(row == rows - 1, high, pltpu.roll(c, rows - 1, 0))
                else:
                    south = jnp.concatenate([low, c[:-1]], axis=0)
                    north = jnp.concatenate([c[1:], high], axis=0)
                put(
                    t,
                    m_ref[0, 0, :, at(t)] * (west - c)
                    + m_ref[1, 0, :, at(t)] * (east - c)
                    + m_ref[2, 0, :, at(t)] * (south - c)
                    + m_ref[3, 0, :, at(t)] * (north - c),
                )

        def put_second(t, x):
            second_ref[:, at(t)] = x

        def put_fourth(t, x):
            fourth_ref[:, at(t)] = x

        def put_out(t, x):
            o_ref[j, 0, :, at(t)] = (
                v_ref[j, 0, :, at(t)] - four_ref[level] * fourth_ref[:, at(t)] + six_ref[level] * x
            )

        laplace(lambda t: v_ref[j, 0, :, at(t)], 0, put_second)
        laplace(lambda t: second_ref[:, at(t)], 1, put_fourth)
        laplace(lambda t: fourth_ref[:, at(t)], 2, put_out)
        return carry

    lax.fori_loop(0, block, one_level, 0)


def damp(fields, damp_four, damp_six, metric, halo_rows, halo_cols):
    levels, faces, rows, width = fields.shape
    block = next(b for b in (4, 2, 1) if levels % b == 0)
    cells = fields.size
    return pl.pallas_call(
        damp_kernel,
        grid=(faces, levels // block),
        in_specs=[
            pl.BlockSpec(memory_space=pltpu.SMEM),
            pl.BlockSpec(memory_space=pltpu.SMEM),
            pl.BlockSpec((block, 1, rows, width), lambda f, l: (l, f, 0, 0)),
            pl.BlockSpec((4, 1, rows, width), lambda f, l: (0, f, 0, 0)),
            pl.BlockSpec((block, 1, 8, width), lambda f, l: (l, f, 0, 0)),
            pl.BlockSpec((1, rows, LANES), lambda f, l: (f, 0, 0)),
        ],
        out_specs=pl.BlockSpec((block, 1, rows, width), lambda f, l: (l, f, 0, 0)),
        out_shape=jax.ShapeDtypeStruct(fields.shape, jnp.float32),
        scratch_shapes=[
            pltpu.VMEM((rows, width), jnp.float32),
            pltpu.VMEM((rows, width), jnp.float32),
        ],
        cost_estimate=pl.CostEstimate(flops=40 * cells, bytes_accessed=10 * cells, transcendentals=0),
        name="damp",
    )(damp_four, damp_six, fields, metric, halo_rows, halo_cols)


def per_device(fields, damp_four, damp_six, metric, seam_table):
    fields = jnp.transpose(fields, (0, 2, 1, 3))
    metric = jnp.transpose(metric, (0, 2, 1, 3))
    levels, faces, rows, width = fields.shape
    rounds = halos_of(fields, metric, seam_table)
    halo_rows = jnp.stack([part for halo in rounds for part in halo[:2]], axis=2)
    halo_rows = jnp.pad(halo_rows, ((0, 0), (0, 0), (0, 2), (0, 0)))
    halo_cols = jnp.stack([part for halo in rounds for part in halo[2:]], axis=0)
    halo_cols = jnp.transpose(halo_cols, (2, 3, 0, 1)).reshape(faces, rows, 6 * levels)
    halo_cols = jnp.pad(halo_cols, ((0, 0), (0, 0), (0, LANES - 6 * levels)))
    damped = damp(fields, damp_four, damp_six, metric, halo_rows, halo_cols)
    return jnp.transpose(damped, (0, 2, 1, 3))


def solution(mesh):
    placed = (
        P("member", "ty", None, None),
        P("member"),
        P("member"),
        P(None, "ty", None, None),
        P(),
    )
    return jax.shard_map(
        per_device,
        mesh=mesh,
        in_specs=placed,
        out_specs=P("member", "ty", None, None),
        check_vma=False,
    )
```
